128 devices in a mesh: blk: 16 (over x_hi, z, core), uly: 8 (over x_lo, y).
Axes of the slice: x: 4 (x_hi: 2, x_lo: 2; x = x_hi * 2 + x_lo), y: 4, z: 4, core: 2. Of those that a mesh axis runs over, the one named last changes fastest.
Arguments:
- queries: bfloat16 [32768, 4096], P(('blk', 'uly')), may hold values from -140 to 140
- keys: bfloat16 [32768, 1024], P(('blk', 'uly')), may hold values from -6 to 6
- values: bfloat16 [32768, 1024], P(('blk', 'uly')), may hold values from -6 to 6
- doc_lengths: int32 [4], replicated, may hold values from 1 to 24576, 32768 in all
- selected: int32 [32, 8], replicated, may hold values from 0 to 30, as said below
Outputs:
- attended: bfloat16 [32768, 4096], P(('blk', 'uly'))
The draws below stay inside these ranges and needn't reach their ends.
Inputs may be any that keep to these rules, and one draw needn't show every extreme that they name: selected[b, g] <= b, and equals b only for b = 0. For every device index along blk (blocks b with equal b // 2) and every key head, the blocks it selects that lie outside its own 2 blocks lie in distinct blocks of blk, so one other index of blk supplies at most one selected block a key head to it.
All inputs are finite; a program needn't handle non-finite values.
Results may differ from the reference program's by a relative error of at most 0.004.
Values may be sent and summed in bfloat16 or wider, within the bound.
A program may use at most 128 MiB of HBM per device.

```python
import math
import jax
import jax.numpy as jnp
import numpy as np
from jax import lax

HQ = 32
KVH = 8
HD = 128
MB = 1024
NDOC = 4
QPD = 2
NQB = 32
TOKENS = 32768
N_BLK = 16


def paired_keys(key):
    base = jax.random.normal(jax.random.fold_in(key, 11), (TOKENS, KVH * HD), jnp.float32)
    return jnp.clip(base, -6.0, 6.0)


def draw_keys(key, part):
    return paired_keys(key).astype(jnp.bfloat16)


def draw_queries(key, part):
    base = jax.random.normal(jax.random.fold_in(key, 12), (TOKENS, HQ * HD), jnp.float32)
    return jnp.clip(base, -6.0, 6.0).astype(jnp.bfloat16)


def draw_selected(key, part):
    block = jnp.arange(NQB, dtype=jnp.int32)
    device = block // QPD
    rank = block % QPD
    places = jnp.arange(N_BLK, dtype=jnp.int32)
    spread = jnp.maximum(places, 1)
    first = jax.random.randint(jax.random.fold_in(key, 21), (N_BLK, KVH), 0, spread[:, None])
    across = (places >= N_BLK // 2)[:, None] & (jnp.arange(KVH, dtype=jnp.int32) == 0)[None, :]
    first = jnp.where(across, (places - N_BLK // 2)[:, None], first)
    within = jax.random.randint(jax.random.fold_in(key, 22), (NQB, KVH), 0, QPD)
    earlier = jax.random.randint(jax.random.fold_in(key, 23), (NQB, KVH), 0, jnp.maximum(rank, 1)[:, None])
    source = (first[device] + rank[:, None]) % jnp.maximum(device, 1)[:, None]
    remote = source * QPD + within
    local = jnp.where(rank[:, None] == 0, block[:, None], device[:, None] * QPD + earlier)
    picked = jnp.where((rank < device)[:, None], remote, local).astype(jnp.int32)
    last_row = (block == NQB - 1)[:, None] & (jnp.arange(KVH, dtype=jnp.int32) == 1)[None, :]
    return jnp.where(last_row, NQB - 2, picked).astype(jnp.int32)


def levels(rng, shape, shards, low, high):
    level, own = 1.0, jax.random.fold_in(rng, 6)
    for position, parts in shards:
        heights = jnp.exp(jax.random.uniform(jax.random.fold_in(own, position), (parts,), jnp.float32, low / len(shards), high / len(shards)))
        level = level * jnp.repeat(heights, shape[position] // parts).reshape([-1 if axis == position else 1 for axis in range(len(shape))])
    return level


def split_up(count, total, bound, lean):
    weights = [(1 << 20) // math.isqrt(rank ** lean) + 1 for rank in range(2, count + 1)]
    rest, holding = total - bound - (count - 1), [1] * (count - 1)
    while rest > 0:
        movable = [i for i in range(count - 1) if holding[i] < bound]
        whole, budget = sum([weights[i] for i in movable]), rest
        for i in movable:
            more = min(bound - holding[i], max(1, budget * weights[i] // whole), rest)
            holding[i] = holding[i] + more
            rest = rest - more
    return np.array([bound] + holding)


def ragged_sizes(key, count, total, bound, lean):
    if count == 2:
        one = jax.random.randint(key, (), max(1, total - bound), min(bound, total - 1) + 1)
        return jnp.stack([one, total - one])
    tallies = jnp.asarray(split_up(count, total, bound, lean), jnp.int32)
    couples = (count - 1) // 2
    donor, sink = tallies[1:1 + 2 * couples:2], tallies[2:2 + 2 * couples:2]
    room = jnp.minimum(donor - 1, bound - sink)
    passed = jax.random.randint(jax.random.fold_in(key, 1), (couples,), 0, 1 << 20) % (room + 1)
    tallies = tallies.at[1:1 + 2 * couples:2].set(donor - passed).at[2:2 + 2 * couples:2].set(sink + passed)
    return tallies[jax.random.permutation(jax.random.fold_in(key, 2), count)]


def centred(key, extent, deviation, limit, pieces=(), kind=jnp.bfloat16):
    array = jax.random.normal(key, extent, jnp.float32) * deviation
    if len(pieces) > 0:
        array = levels(key, extent, pieces, -0.22, 0.18) * array
    return jnp.clip(array, min=-limit, max=limit).astype(kind)


def setup_inputs(seed: int = 0) -> dict:
    key_of = jax.random.split(jax.random.key(seed), 6)
    return {
        "queries": draw_queries(jax.random.fold_in(key_of[5], 71), 0),
        "keys": draw_keys(jax.random.fold_in(key_of[5], 71), 0),
        "values": centred(key_of[2], (TOKENS, KVH * HD), 1.0, 6.0, ((0, 128),)),
        "doc_lengths": ragged_sizes(key_of[3], NDOC, TOKENS, 3 * TOKENS // 4, 2).astype(jnp.int32),
        "selected": draw_selected(jax.random.fold_in(key_of[5], 71), 0),
    }


def reference(queries, keys, values, doc_lengths, selected):
    group = HQ // KVH
    scale = 1.0 / (HD ** 0.5)
    ends = jnp.cumsum(doc_lengths)
    places = jnp.arange(TOKENS, dtype=jnp.int32)
    doc = jnp.sum((ends[None, :] <= places[:, None]).astype(jnp.int32), axis=1).reshape(NQB, MB)
    q_five = queries.reshape(NQB, MB, KVH, group, HD)
    k_four = keys.reshape(NQB, MB, KVH, HD)
    v_four = values.reshape(NQB, MB, KVH, HD)
    heads = jnp.arange(KVH, dtype=jnp.int32)
    line = jnp.arange(MB, dtype=jnp.int32)
    causal = line[:, None] >= line[None, :]

    def one_block(block):
        q_now = q_five[block].astype(jnp.float32)
        picks = selected[block]
        k_own = jnp.transpose(k_four[block], (1, 0, 2))
        v_own = jnp.transpose(v_four[block], (1, 0, 2))
        k_sel = k_four[picks, :, heads]
        v_sel = v_four[picks, :, heads]
        k_all = jnp.concatenate([k_own, k_sel], axis=1).astype(jnp.float32)
        v_all = jnp.concatenate([v_own, v_sel], axis=1).astype(jnp.float32)
        scores = jnp.einsum("mhgd,hnd->hgmn", q_now, k_all) * scale
        doc_q = doc[block]
        doc_s = doc[picks]
        own_mask = causal & (doc_q[:, None] == doc_q[None, :])
        own_mask = jnp.broadcast_to(own_mask[None], (KVH, MB, MB))
        sel_mask = (doc_q[None, :, None] == doc_s[:, None, :]) & (picks != block)[:, None, None]
        mask = jnp.concatenate([own_mask, sel_mask], axis=2)[:, None]
        top = jnp.max(jnp.where(mask, scores, -jnp.inf), axis=-1, keepdims=True)
        weight = jnp.where(mask, jnp.exp(scores - top), 0.0)
        total = jnp.sum(weight, axis=-1)
        rounded = lax.optimization_barrier(weight.astype(jnp.bfloat16)).astype(jnp.float32)
        acc = jnp.einsum("hgmn,hnd->mhgd", rounded, v_all)
        out = acc / jnp.transpose(total, (2, 0, 1))[..., None]
        return out.astype(jnp.bfloat16).reshape(MB, HQ * HD)

    return lax.map(one_block, jnp.arange(NQB, dtype=jnp.int32)).reshape(TOKENS, HQ * HD)
```

```python
import functools
import math

import jax
import jax.numpy as jnp
from jax import lax
from jax.experimental import pallas as pl
from jax.experimental.pallas import tpu as pltpu
from jax.sharding import PartitionSpec as P

HQ = 32
KVH = 8
HD = 128
NY = 4
GROUP = HQ // KVH
HEADS = KVH // NY
BIG = float(1 << 20)
LOG2E_SCALE = math.log2(math.e) / math.sqrt(HD)
MESH = pl.DeviceIdType.MESH


def device(x, y, z, c):
    return ((x // 2) * 8 + z * 2 + c, (x % 2) * NY + y)


def kernel(
    rows,
    q_hbm,
    k_hbm,
    v_hbm,
    lengths,
    selected,
    out_hbm,
    q_all,
    kv_own,
    gathered_0,
    gathered_1,
    picked,
    arrived_0,
    arrived_1,
    k_aug,
    v_aug,
    q_doc,
    acc_ref,
    top_ref,
    out_all,
    kv_send,
    kv_recv,
    q_send,
    q_recv,
    pre_send,
    pre_recv,
    a_send,
    a_recv,
    b_send,
    b_recv,
    o_send,
    o_recv,
    local_kv,
    local_q,
    local_g,
    local_o,
):
    block = NY * rows
    half = block // 2
    gathered, arrived = (gathered_0, gathered_1), (arrived_0, arrived_1)
    blk, uly = lax.axis_index("blk"), lax.axis_index("uly")
    xh, z, c = blk // 8, (blk // 2) % 4, blk % 2
    xl, y = uly // NY, uly % NY
    x = xh * 2 + xl
    a = x * (1 - c) + z * c
    b = z * (1 - c) + x * c
    a_other = z * (1 - c) + x * c
    partner = device(x, y, z, 1 - c)

    def along_a(a_to):
        return device(a_to * (1 - c) + x * c, y, z * (1 - c) + a_to * c, c)

    def along_b(b_to, c_to):
        return device(x * (1 - c) + b_to * c, y, b_to * (1 - c) + z * c, c_to)

    def remote(src, dst, send, recv, to):
        return pltpu.make_async_remote_copy(
            src_ref=src, dst_ref=dst, send_sem=send, recv_sem=recv, device_id=to, device_id_type=MESH
        )

    barrier = pltpu.get_barrier_semaphore()
    friends = [partner] + [device(x, (y + k) % 4, z, c) for k in (1, 2, 3)]
    for k in (1, 2, 3):
        for core in (0, 1):
            friends.append(device((x + k) % 4, y, z, core))
            friends.append(device(x, y, (z + k) % 4, core))
    for friend in friends:
        pl.semaphore_signal(barrier, inc=1, device_id=friend, device_id_type=MESH)
    pl.semaphore_wait(barrier, len(friends))

    def kv_copy(h, kv, k):
        to = (y + k) % 4
        columns = pl.ds(pl.multiple_of((to * HEADS + h) * HD, HD), HD)
        src = (k_hbm if kv == 0 else v_hbm).at[:, columns]
        dst = kv_own.at[h, kv, pl.ds(pl.multiple_of(y * rows, rows), rows)]
        if k == 0:
            return pltpu.make_async_copy(src, dst, local_kv.at[h, kv])
        return remote(src, dst, kv_send.at[h, kv, k - 1], kv_recv.at[h, kv, k - 1], device(x, to, z, c))

    def q_copy(h, k):
        to = (y + k) % 4
        width = GROUP * HD
        columns = pl.ds(pl.multiple_of((to * HEADS + h) * width, width), width)
        src, dst = q_hbm.at[:, columns], q_all.at[h, y]
        if k == 0:
            return pltpu.make_async_copy(src, dst, local_q.at[h])
        return remote(src, dst, q_send.at[h, k - 1], q_recv.at[h, k - 1], device(x, to, z, c))

    def out_copy(h, t, k):
        width = GROUP * HD
        columns = pl.ds(pl.multiple_of((y * HEADS + h) * width, width), width)
        src, dst = out_all.at[h, t], out_hbm.at[:, columns]
        if k == 0:
            return pltpu.make_async_copy(src, dst, local_o.at[h])
        return remote(src, dst, o_send.at[h, k - 1], o_recv.at[h, k - 1], device(x, t, z, c))

    my_rows = pl.ds(pl.multiple_of(c * half, half), half)
    other_rows = pl.ds(pl.multiple_of((1 - c) * half, half), half)

    def pre_copy(h):
        return remote(
            kv_own.at[h, :, other_rows],
            gathered[h].at[a_other * 2 + c],
            pre_send.at[h],
            pre_recv.at[h],
            partner,
        )

    def own_half(h):
        return pltpu.make_async_copy(kv_own.at[h, :, my_rows], gathered[h].at[a * 2 + c], local_g.at[h])

    def a_copy(h, own, k):
        slot = a * 2 + (c if own else 1 - c)
        src = kv_own.at[h, :, my_rows] if own else gathered[h].at[slot]
        index = 0 if own else 1
        return remote(
            src,
            gathered[h].at[slot],
            a_send.at[h, index, k - 1],
            a_recv.at[h, index, k - 1],
            along_a((a + k) % 4),
        )

    def b_copy(h, core, k):
        return remote(
            picked.at[h, core, k],
            arrived[h].at[c, b],
            b_send.at[h, core, k],
            b_recv.at[h, c, k],
            along_b((b + k) % 4, core),
        )

    def b_partner(h):
        return remote(
            picked.at[h, 0, 0],
            arrived[h].at[c, b],
            b_send.at[h, 0, 0],
            b_recv.at[h, c, 0],
            partner,
        )

    def b_wait(h, r, k):
        slot = ((z if r == 0 else x) - k + 4) % 4
        remote(
            picked.at[h, 0, 0],
            arrived[h].at[r, slot],
            b_send.at[h, 0, 0],
            b_recv.at[h, r, k],
            partner,
        ).wait_recv()

    def wanted(x_to, z_to, c_to, h):
        place = (x_to // 2) * 16 + z_to * 4 + c_to * 2 + x_to % 2
        pick = selected[place, y * HEADS + h]
        return pick, (pick // 16) * 2 + pick % 2, (pick // 4) % 4, (pick // 2) % 2

    def choose(h, x_to, z_to, c_to):
        _, x_s, z_s, c_s = wanted(x_to, z_to, c_to, h)
        return gathered[h][(x_s * (1 - c) + z_s * c) * 2 + c_s]

    lane = lax.broadcasted_iota(jnp.int32, (1, HD), 1)
    begin = jnp.zeros((1, HD), jnp.int32)
    end = jnp.full((1, HD), 1 << 30, jnp.int32)
    total = jnp.int32(0)
    for d in range(4):
        begin = jnp.where(lane == d, total, begin)
        total = total + lengths[d]
        end = jnp.where(lane == d, total, end)

    place_me = xh * 16 + z * 4 + c * 2 + xl

    def inside(first, n):
        p = first + lax.broadcasted_iota(jnp.int32, (n, HD), 0)
        return (p >= begin) & (p < end)

    def penalty(first, n, live):
        visible = inside(first, n)
        hidden = jnp.where(live, 0.0, -BIG)
        return jnp.where(visible, hidden, -BIG).astype(jnp.bfloat16)

    def scores(q_tile, keys):
        return lax.dot_general(
            q_tile, keys, (((1,), (1,)), ((), ())), preferred_element_type=jnp.float32
        )

    def query(h, t, j):
        return jnp.concatenate(
            [q_all[h, t, :, j * HD : (j + 1) * HD], q_doc[pl.ds(pl.multiple_of(t * rows, rows), rows)]], axis=1
        )

    def own_setup(h):
        k_aug[h, 0, :, :HD] = kv_own[h, 0]
        k_aug[h, 0, :, HD:] = penalty(place_me * block, block, True)
        v_aug[h, 0, :, :HD] = kv_own[h, 1]
        v_aug[h, 0, :, HD:] = jnp.ones((block, HD), jnp.bfloat16)

    def own_attention(h):
        row = lax.broadcasted_iota(jnp.int32, (rows, rows), 0)
        column = lax.broadcasted_iota(jnp.int32, (rows, rows), 1)
        for t in range(NY):
            for j in range(GROUP):
                q_tile = query(h, t, j)
                last = scores(q_tile, k_aug[h, 0, t * rows : (t + 1) * rows])
                last = jnp.where(row >= column, last, -BIG)
                top = jnp.max(last, axis=1, keepdims=True)
                if t > 0:
                    first = scores(q_tile, k_aug[h, 0, : t * rows])
                    top = jnp.maximum(top, jnp.max(first, axis=1, keepdims=True))
                weight = jnp.exp2((last - top) * LOG2E_SCALE).astype(jnp.bfloat16)
                acc = jnp.dot(
                    weight, v_aug[h, 0, t * rows : (t + 1) * rows], preferred_element_type=jnp.float32
                )
                if t > 0:
                    weight = jnp.exp2((first - top) * LOG2E_SCALE).astype(jnp.bfloat16)
                    acc = acc + jnp.dot(weight, v_aug[h, 0, : t * rows], preferred_element_type=jnp.float32)
                acc_ref[h, t, j] = acc
                top_ref[h, t, j] = jnp.broadcast_to(top, (rows, HD))

    def sel_setup(h):
        pick, x_s, z_s, _ = wanted(x, z, c, h)
        live = pick != place_me
        for r, slot in ((0, z_s), (1, x_s)):
            there = slice(r * half, (r + 1) * half)
            both = arrived[h][r, slot]
            k_aug[h, 1, there, :HD] = both[0]
            k_aug[h, 1, there, HD:] = penalty(pick * block + r * half, half, live)
            v_aug[h, 1, there, :HD] = both[1]
            v_aug[h, 1, there, HD:] = jnp.ones((half, HD), jnp.bfloat16)

    def sel_attention(h, t):
        for j in range(GROUP):
            s = scores(query(h, t, j), k_aug[h, 1])
            before = top_ref[h, t, j][:, :1]
            top = jnp.maximum(before, jnp.max(s, axis=1, keepdims=True))
            weight = jnp.exp2((s - top) * LOG2E_SCALE).astype(jnp.bfloat16)
            acc = jnp.dot(weight, v_aug[h, 1], preferred_element_type=jnp.float32)
            acc = acc + acc_ref[h, t, j] * jnp.exp2((before - top) * LOG2E_SCALE)
            out_all[h, t, :, j * HD : (j + 1) * HD] = (acc[:, :HD] / acc[:, HD:]).astype(jnp.bfloat16)

    for h in range(HEADS):
        for k in (2, 1, 3, 0):
            for kv in (0, 1):
                kv_copy(h, kv, k).start()
    for h in range(HEADS):
        for k in (2, 1, 3, 0):
            q_copy(h, k).start()
    q_doc[...] = jnp.where(inside(place_me * block, block), 1.0, 0.0).astype(jnp.bfloat16)

    for h in range(HEADS):
        for kv in (0, 1):
            kv_copy(h, kv, 0).wait()
            for k in (1, 2, 3):
                kv_copy(h, kv, k).wait_recv()
        pre_copy(h).start()
        for k in (2, 1, 3):
            a_copy(h, True, k).start()
        own_half(h).start()
        own_setup(h)
        pre_copy(h).wait_recv()
        for k in (2, 1, 3):
            a_copy(h, False, k).start()

    for h in range(HEADS):
        own_half(h).wait()
        for index in (True, False):
            for k in (1, 2, 3):
                a_copy(h, index, k).wait_recv()
        for k in (2, 1, 3):
            b_to = (b + k) % 4
            for core in (0, 1):
                picked[h, core, k] = choose(h, x * (1 - c) + b_to * c, b_to * (1 - c) + z * c, core)
                b_copy(h, core, k).start()
        picked[h, 0, 0] = choose(h, x, z, 1 - c)
        b_partner(h).start()
        arrived[h][c, b] = choose(h, x, z, c)
        q_copy(h, 0).wait()
        for k in (1, 2, 3):
            q_copy(h, k).wait_recv()
        own_attention(h)

    for h in range(HEADS):
        for k in (1, 2, 3):
            b_wait(h, 0, k)
            b_wait(h, 1, k)
        b_back = remote(
            picked.at[h, 0, 0],
            arrived[h].at[1 - c, z * c + x * (1 - c)],
            b_send.at[h, 0, 0],
            b_recv.at[h, 1 - c, 0],
            partner,
        )
        b_back.wait_recv()
        sel_setup(h)
        for k in (2, 1, 3, 0):
            t = (y + k) % 4
            sel_attention(h, t)
            out_copy(h, t, k).start()

    for h in range(HEADS):
        for k in (1, 2, 3):
            for kv in (0, 1):
                kv_copy(h, kv, k).wait_send()
            q_copy(h, k).wait_send()
            a_copy(h, True, k).wait_send()
            a_copy(h, False, k).wait_send()
            b_copy(h, 0, k).wait_send()
            b_copy(h, 1, k).wait_send()
        pre_copy(h).wait_send()
        b_partner(h).wait_send()
        out_copy(h, y, 0).wait()
        for k in (1, 2, 3):
            out_copy(h, (y + k) % 4, k).wait_send()
            out_copy(h, (y + k) % 4, k).wait_recv()


def on_device(queries, keys, values, doc_lengths, selected):
    rows = queries.shape[0]
    block = NY * rows
    half = block // 2
    width = GROUP * HD
    bf16, f32 = jnp.bfloat16, jnp.float32
    dma = pltpu.SemaphoreType.DMA
    anywhere = pl.BlockSpec(memory_space=pl.ANY)
    scalars = pl.BlockSpec(memory_space=pltpu.SMEM)
    return pl.pallas_call(
        functools.partial(kernel, rows),
        out_shape=jax.ShapeDtypeStruct(queries.shape, bf16),
        in_specs=[anywhere, anywhere, anywhere, scalars, scalars],
        out_specs=anywhere,
        scratch_shapes=[
            pltpu.VMEM((HEADS, NY, rows, width), bf16),
            pltpu.VMEM((HEADS, 2, block, HD), bf16),
            pltpu.VMEM((8, 2, half, HD), bf16),
            pltpu.VMEM((8, 2, half, HD), bf16),
            pltpu.VMEM((HEADS, 2, 4, 2, half, HD), bf16),
            pltpu.VMEM((2, 4, 2, half, HD), bf16),
            pltpu.VMEM((2, 4, 2, half, HD), bf16),
            pltpu.VMEM((HEADS, 2, block, 2 * HD), bf16),
            pltpu.VMEM((HEADS, 2, block, 2 * HD), bf16),
            pltpu.VMEM((block, HD), bf16),
            pltpu.VMEM((HEADS, NY, GROUP, rows, 2 * HD), f32),
            pltpu.VMEM((HEADS, NY, GROUP, rows, HD), f32),
            pltpu.VMEM((HEADS, NY, rows, width), bf16),
            dma((HEADS, 2, 3)),
            dma((HEADS, 2, 3)),
            dma((HEADS, 3)),
            dma((HEADS, 3)),
            dma((HEADS,)),
            dma((HEADS,)),
            dma((HEADS, 2, 3)),
            dma((HEADS, 2, 3)),
            dma((HEADS, 2, 4)),
            dma((HEADS, 2, 4)),
            dma((HEADS, 3)),
            dma((HEADS, 3)),
            dma((HEADS, 2)),
            dma((HEADS,)),
            dma((HEADS,)),
            dma((HEADS,)),
        ],
        compiler_params=pltpu.CompilerParams(
            collective_id=0, has_side_effects=True, vmem_limit_bytes=60 * 1024 * 1024
        ),
        name="exchange_and_attend",
    )(queries, keys, values, doc_lengths, selected)


def solution(mesh):
    rows = P(("blk", "uly"), None)
    return jax.shard_map(
        on_device, mesh=mesh, in_specs=(rows, rows, rows, P(), P()), out_specs=rows, check_vma=False
    )
```

```python
import functools
import math

import jax
import jax.numpy as jnp
from jax import lax
from jax.experimental import pallas as pl
from jax.experimental.pallas import tpu as pltpu
from jax.sharding import PartitionSpec as P

HQ = 32
KVH = 8
HD = 128
NY = 4
GROUP = HQ // KVH
HEADS = KVH // NY
BIG = float(1 << 20)
LOG2E_SCALE = math.log2(math.e) / math.sqrt(HD)
MESH = pl.DeviceIdType.MESH


def device(x, y, z, c):
    return ((x // 2) * 8 + z * 2 + c, (x % 2) * NY + y)


def kernel(
    rows,
    q_hbm,
    k_hbm,
    v_hbm,
    lengths,
    selected,
    out_hbm,
    q_all,
    kv_own,
    gathered_00,
    gathered_01,
    gathered_10,
    gathered_11,
    relayed_00,
    relayed_01,
    relayed_10,
    relayed_11,
    picked,
    final,
    arrived_0,
    arrived_1,
    k_aug,
    v_aug,
    q_doc,
    acc_ref,
    top_ref,
    out_all,
    kv_send,
    kv_recv,
    q_send,
    q_recv,
    pre_send,
    pre_recv,
    a_send,
    a_recv,
    b_send,
    b_recv,
    c_recv,
    o_send,
    o_recv,
    local_kv,
    local_q,
    local_g,
    local_o,
):
    block = NY * rows
    quarter = rows // 4
    gathered = ((gathered_00, gathered_01), (gathered_10, gathered_11))
    relayed = ((relayed_00, relayed_01), (relayed_10, relayed_11))
    arrived = (arrived_0, arrived_1)
    blk, uly = lax.axis_index("blk"), lax.axis_index("uly")
    xh, z, c = blk // 8, (blk // 2) % 4, blk % 2
    xl, y = uly // NY, uly % NY
    x = xh * 2 + xl
    a = x * (1 - c) + z * c
    b = z * (1 - c) + x * c
    partner = device(x, y, z, 1 - c)

    def along_a(a_to):
        return device(a_to * (1 - c) + x * c, y, z * (1 - c) + a_to * c, c)

    def along_b(b_to, c_to):
        return device(x * (1 - c) + b_to * c, y, b_to * (1 - c) + z * c, c_to)

    def remote(src, dst, send, recv, to):
        return pltpu.make_async_remote_copy(
            src_ref=src, dst_ref=dst, send_sem=send, recv_sem=recv, device_id=to, device_id_type=MESH
        )

    barrier = pltpu.get_barrier_semaphore()
    friends = [partner] + [device(x, (y + k) % 4, z, c) for k in (1, 2, 3)]
    for k in (1, 3):
        for core in (0, 1):
            friends.append(device((x + k) % 4, y, z, core))
            friends.append(device(x, y, (z + k) % 4, core))
    for friend in friends:
        pl.semaphore_signal(barrier, inc=1, device_id=friend, device_id_type=MESH)

    def kv_copy(h, kv, k):
        to = (y + k) % 4
        columns = pl.ds(pl.multiple_of((to * HEADS + h) * HD, HD), HD)
        src = (k_hbm if kv == 0 else v_hbm).at[:, :, columns]
        dst = kv_own.at[h, :, kv, y]
        if k == 0:
            return pltpu.make_async_copy(src, dst, local_kv.at[h, kv])
        return remote(src, dst, kv_send.at[h, kv, k - 1], kv_recv.at[h, kv, k - 1], device(x, to, z, c))

    def q_copy(h, k):
        to = (y + k) % 4
        width = GROUP * HD
        columns = pl.ds(pl.multiple_of((to * HEADS + h) * width, width), width)
        src, dst = q_hbm.at[:, columns], q_all.at[h, y]
        if k == 0:
            return pltpu.make_async_copy(src, dst, local_q.at[h])
        return remote(src, dst, q_send.at[h, k - 1], q_recv.at[h, k - 1], device(x, to, z, c))

    def out_copy(h, t, k):
        width = GROUP * HD
        columns = pl.ds(pl.multiple_of((y * HEADS + h) * width, width), width)
        src, dst = out_all.at[h, t], out_hbm.at[:, columns]
        if k == 0:
            return pltpu.make_async_copy(src, dst, local_o.at[h])
        return remote(src, dst, o_send.at[h, k - 1], o_recv.at[h, k - 1], device(x, t, z, c))

    def near(p):
        return p + 1 - 2 * (p % 2)

    def far(p):
        return 3 - p

    def pairing(j, step):
        return (near, far)[(j + step) % 2]

    def source(k):
        return (y - k + 4) % 4

    def pre_copy(h, j, k):
        chunk = source(k)
        return remote(
            kv_own.at[h, 2 * (1 - c) + j, :, chunk],
            gathered[h][j].at[b * 2 + c, :, chunk],
            pre_send.at[h, j, k],
            pre_recv.at[h, j, k],
            partner,
        )

    def own_item(h, j):
        return pltpu.make_async_copy(kv_own.at[h, 2 * c + j], gathered[h][j].at[a * 2 + c], local_g.at[h, j])

    def first_copy(h, j, own, k=None):
        slot = a * 2 + (c if own else 1 - c)
        src = kv_own.at[h, 2 * c + j] if own else gathered[h][j].at[slot]
        dst = gathered[h][j].at[slot]
        if k is not None:
            src, dst = src.at[:, source(k)], dst.at[:, source(k)]
        index = 0 if own else 1
        return remote(
            src,
            dst,
            a_send.at[h, j, index],
            a_recv.at[h, j, index],
            along_a(pairing(j, 0)(a)),
        )

    def second_copy(h, j, own):
        place = a if own else pairing(j, 0)(a)
        pair = pl.ds(place * 2, 2)
        index = 2 if own else 3
        return remote(
            gathered[h][j].at[pair],
            gathered[h][j].at[pair],
            a_send.at[h, j, index],
            a_recv.at[h, j, index],
            along_a(pairing(j, 1)(a)),
        )

    def third_copy(h, j):
        return remote(
            picked.at[h, j], relayed[h][j], b_send.at[h, j, 0], b_recv.at[h, j, 0], along_b(pairing(j, 0)(b), c)
        )

    def fourth_copy(h, j, core):
        return remote(
            final.at[h, j, core],
            arrived[h].at[2 * c + j, 1],
            b_send.at[h, j, 1 + core],
            c_recv.at[h, 2 * c + j, 1],
            along_b(pairing(j, 1)(b), core),
        )

    def partner_copy(h, j):
        return remote(
            final.at[h, j, 2],
            arrived[h].at[2 * c + j, 0],
            b_send.at[h, j, 3],
            c_recv.at[h, 2 * c + j, 0],
            partner,
        )

    def arrival(h, unit, slot):
        return remote(
            final.at[h, 0, 0], arrived[h].at[unit, slot], b_send.at[h, 0, 1], c_recv.at[h, unit, slot], partner
        )

    def wanted(x_to, z_to, c_to, h):
        place = (x_to // 2) * 16 + z_to * 4 + c_to * 2 + x_to % 2
        pick = selected[y * HEADS + h, place]
        return pick, (pick // 16) * 2 + pick % 2, (pick // 4) % 4, (pick // 2) % 2

    def request(h, b_to, c_to):
        x_to, z_to = x * (1 - c) + b_to * c, b_to * (1 - c) + z * c
        _, x_s, z_s, c_s = wanted(x_to, z_to, c_to, h)
        return (x_s * (1 - c) + z_s * c) * 2 + c_s, z_s * (1 - c) + x_s * c

    def pick_third(h, j):
        to = pairing(j, 0)(b)
        for w, b_to in ((0, to), (1, pairing(j, 1)(to))):
            for core in (0, 1):
                picked[h, j, 2 * w + core] = gathered[h][j][request(h, b_to, core)[0]]

    def pick_fourth(h, j, w, core):
        b_to = pairing(j, 1)(b) if w else b
        index, b_s = request(h, b_to, core)
        return jnp.where(b_s == b, gathered[h][j][index], relayed[h][j][2 * w + core])

    lane = lax.broadcasted_iota(jnp.int32, (1, HD), 1)
    begin = jnp.zeros((1, HD), jnp.int32)
    end = jnp.full((1, HD), 1 << 30, jnp.int32)
    total = jnp.int32(0)
    for d in range(4):
        begin = jnp.where(lane == d, total, begin)
        total = total + lengths[d]
        end = jnp.where(lane == d, total, end)

    place_me = xh * 16 + z * 4 + c * 2 + xl

    def inside(first, n):
        p = first + lax.broadcasted_iota(jnp.int32, (n, HD), 0)
        return (p >= begin) & (p < end)

    def penalty(first, live, regrouped):
        i = lax.broadcasted_iota(jnp.int32, (block, HD), 0)
        if regrouped:
            i = (i // quarter % NY) * rows + (i // rows) * quarter + i % quarter
        p = first + i
        visible = (p >= begin) & (p < end)
        hidden = jnp.where(live, 0.0, -BIG)
        return jnp.where(visible, hidden, -BIG).astype(jnp.bfloat16)

    def scores(q_tile, keys):
        return lax.dot_general(
            q_tile, keys, (((1,), (1,)), ((), ())), preferred_element_type=jnp.float32
        )

    def query(h, t, j):
        return jnp.concatenate(
            [q_all[h, t, :, j * HD : (j + 1) * HD], q_doc[pl.ds(pl.multiple_of(t * rows, rows), rows)]], axis=1
        )

    def own_setup(h):
        for chunk in range(NY):
            for unit in range(4):
                there = slice(chunk * rows + unit * quarter, chunk * rows + (unit + 1) * quarter)
                k_aug[h, 0, there, :HD] = kv_own[h, unit, 0, chunk]
                v_aug[h, 0, there, :HD] = kv_own[h, unit, 1, chunk]
        k_aug[h, 0, :, HD:] = penalty(place_me * block, True, False)
        v_aug[h, 0, :, HD:] = jnp.ones((block, HD), jnp.bfloat16)

    def own_attention(h, tiles):
        row = lax.broadcasted_iota(jnp.int32, (rows, rows), 0)
        column = lax.broadcasted_iota(jnp.int32, (rows, rows), 1)
        for t in tiles:
            for j in range(GROUP):
                q_tile = query(h, t, j)
                last = scores(q_tile, k_aug[h, 0, t * rows : (t + 1) * rows])
                last = jnp.where(row >= column, last, -BIG)
                top = jnp.max(last, axis=1, keepdims=True)
                if t > 0:
                    first = scores(q_tile, k_aug[h, 0, : t * rows])
                    top = jnp.maximum(top, jnp.max(first, axis=1, keepdims=True))
                weight = jnp.exp2((last - top) * LOG2E_SCALE).astype(jnp.bfloat16)
                acc = jnp.dot(
                    weight, v_aug[h, 0, t * rows : (t + 1) * rows], preferred_element_type=jnp.float32
                )
                if t > 0:
                    weight = jnp.exp2((first - top) * LOG2E_SCALE).astype(jnp.bfloat16)
                    acc = acc + jnp.dot(weight, v_aug[h, 0, : t * rows], preferred_element_type=jnp.float32)
                acc_ref[h, t, j] = acc
                top_ref[h, t, j] = jnp.broadcast_to(top, (rows, HD))

    def sel_setup(h):
        pick, x_s, z_s, _ = wanted(x, z, c, h)
        live = pick != place_me
        for r, source, here in ((0, z_s, z), (1, x_s, x)):
            for j in (0, 1):
                unit = 2 * r + j
                slot = jnp.where((source == here) | (source == pairing(j, 0)(here)), 0, 1)
                both = arrived[h][unit, slot]
                there = slice(unit * rows, (unit + 1) * rows)
                k_aug[h, 1, there, :HD] = both[0].reshape(rows, HD)
                v_aug[h, 1, there, :HD] = both[1].reshape(rows, HD)
        k_aug[h, 1, :, HD:] = penalty(pick * block, live, True)
        v_aug[h, 1, :, HD:] = jnp.ones((block, HD), jnp.bfloat16)

    def sel_attention(h, t):
        for j in range(GROUP):
            s = scores(query(h, t, j), k_aug[h, 1])
            before = top_ref[h, t, j][:, :1]
            top = jnp.maximum(before, jnp.max(s, axis=1, keepdims=True))
            weight = jnp.exp2((s - top) * LOG2E_SCALE).astype(jnp.bfloat16)
            acc = jnp.dot(weight, v_aug[h, 1], preferred_element_type=jnp.float32)
            acc = acc + acc_ref[h, t, j] * jnp.exp2((before - top) * LOG2E_SCALE)
            out_all[h, t, :, j * HD : (j + 1) * HD] = (acc[:, :HD] / acc[:, HD:]).astype(jnp.bfloat16)

    for h in range(HEADS):
        for kv in (0, 1):
            kv_copy(h, kv, 0).start()
    for h in range(HEADS):
        q_copy(h, 0).start()
    q_doc[...] = jnp.where(inside(place_me * block, block), 1.0, 0.0).astype(jnp.bfloat16)
    pl.semaphore_wait(barrier, len(friends))

    def send_keys(h):
        for k in (1, 3, 2):
            for kv in (0, 1):
                if h > 0:
                    kv_copy(h - 1, kv, k).wait_send()
                kv_copy(h, kv, k).start()

    def send_queries(h):
        for k in (1, 3, 2):
            if h == 0:
                for kv in (0, 1):
                    kv_copy(HEADS - 1, kv, k).wait_send()
            else:
                q_copy(h - 1, k).wait_send()
            q_copy(h, k).start()

    def send_first(h, k):
        for kv in (0, 1):
            if k == 0:
                kv_copy(h, kv, k).wait()
            else:
                kv_copy(h, kv, k).wait_recv()
        for j in (0, 1):
            pre_copy(h, j, k).start()
        for j in (0, 1):
            first_copy(h, j, True, k).start()

    def pass_first(h, k):
        for j in (0, 1):
            pre_copy(h, j, k).wait_recv()
            first_copy(h, j, False, k).start()

    def send_second_own(h):
        for j in (0, 1):
            own_item(h, j).start()
        for j in (0, 1):
            own_item(h, j).wait()
            second_copy(h, j, True).start()

    def send_second(h):
        for j in (0, 1):
            first_copy(h, j, True).wait_recv()
            first_copy(h, j, False).wait_recv()
            second_copy(h, j, False).start()

    def send_third(h):
        for j in (0, 1):
            second_copy(h, j, True).wait_recv()
            second_copy(h, j, False).wait_recv()
            pick_third(h, j)
            third_copy(h, j).start()

    def send_fourth(h):
        for j in (0, 1):
            third_copy(h, j).wait_recv()
            for core in (0, 1):
                final[h, j, core] = pick_fourth(h, j, 1, core)
                fourth_copy(h, j, core).start()
        for j in (0, 1):
            final[h, j, 2] = jnp.where(c == 0, pick_fourth(h, j, 0, 1), pick_fourth(h, j, 0, 0))
            partner_copy(h, j).start()
            arrived[h][2 * c + j, 0] = jnp.where(c == 0, pick_fourth(h, j, 0, 0), pick_fourth(h, j, 0, 1))

    def queries_here(h):
        q_copy(h, 0).wait()
        for k in (1, 2, 3):
            q_copy(h, k).wait_recv()

    def finish(h):
        for unit in range(4):
            arrival(h, unit, 1).wait_recv()
        for j in (0, 1):
            arrival(h, 2 * (1 - c) + j, 0).wait_recv()
        sel_setup(h)
        for k in (2, 1, 3, 0):
            t = (y + k) % 4
            sel_attention(h, t)
            out_copy(h, t, k).start()

    send_keys(0)
    for h in range(HEADS):
        send_first(h, 0)
    for h in range(HEADS):
        pass_first(h, 0)
    send_keys(1)
    for k in (1, 3, 2):
        send_first(0, k)
        pass_first(0, k)
    send_second_own(0)
    send_queries(0)
    own_setup(0)
    send_second(0)
    for k in (1, 3, 2):
        send_first(1, k)
        pass_first(1, k)
    send_second_own(1)
    own_setup(1)
    send_third(0)
    send_queries(1)
    for j in (0, 1):
        third_copy(0, j).wait_send()
    send_second(1)
    queries_here(0)
    own_attention(0, (0, 1))
    send_fourth(0)
    own_attention(0, (2, 3))
    send_third(1)
    finish(0)
    queries_here(1)
    own_attention(1, (0, 1, 2))
    send_fourth(1)
    own_attention(1, (3,))
    finish(1)

    for h in range(HEADS):
        for j in (0, 1):
            for k in range(NY):
                pre_copy(h, j, k).wait_send()
            for own in (True, False):
                first_copy(h, j, own).wait_send()
                second_copy(h, j, own).wait_send()
            if h > 0:
                third_copy(h, j).wait_send()
            for core in (0, 1):
                fourth_copy(h, j, core).wait_send()
            partner_copy(h, j).wait_send()
        out_copy(h, y, 0).wait()
        for k in (1, 2, 3):
            if h > 0:
                q_copy(h, k).wait_send()
            out_copy(h, (y + k) % 4, k).wait_send()
            out_copy(h, (y + k) % 4, k).wait_recv()


def on_device(queries, keys, values, doc_lengths, selected):
    rows = queries.shape[0]
    block = NY * rows
    item = (2, NY, rows // 4, HD)
    width = GROUP * HD
    split = (4, rows // 4, keys.shape[1])
    bf16, f32 = jnp.bfloat16, jnp.float32
    dma = pltpu.SemaphoreType.DMA
    anywhere = pl.BlockSpec(memory_space=pl.ANY)
    scalars = pl.BlockSpec(memory_space=pltpu.SMEM)
    return pl.pallas_call(
        functools.partial(kernel, rows),
        out_shape=jax.ShapeDtypeStruct(queries.shape, bf16),
        in_specs=[anywhere, anywhere, anywhere, scalars, scalars],
        out_specs=anywhere,
        scratch_shapes=[
            pltpu.VMEM((HEADS, NY, rows, width), bf16),
            pltpu.VMEM((HEADS, 4) + item, bf16),
            *[pltpu.VMEM((8,) + item, bf16)] * 4,
            *[pltpu.VMEM((4,) + item, bf16)] * 4,
            pltpu.VMEM((HEADS, 2, 4) + item, bf16),
            pltpu.VMEM((HEADS, 2, 3) + item, bf16),
            *[pltpu.VMEM((4, 2) + item, bf16)] * 2,
            pltpu.VMEM((HEADS, 2, block, 2 * HD), bf16),
            pltpu.VMEM((HEADS, 2, block, 2 * HD), bf16),
            pltpu.VMEM((block, HD), bf16),
            pltpu.VMEM((HEADS, NY, GROUP, rows, 2 * HD), f32),
            pltpu.VMEM((HEADS, NY, GROUP, rows, HD), f32),
            pltpu.VMEM((HEADS, NY, rows, width), bf16),
            dma((HEADS, 2, 3)),
            dma((HEADS, 2, 3)),
            dma((HEADS, 3)),
            dma((HEADS, 3)),
            dma((HEADS, 2, NY)),
            dma((HEADS, 2, NY)),
            dma((HEADS, 2, 4)),
            dma((HEADS, 2, 4)),
            dma((HEADS, 2, 4)),
            dma((HEADS, 2, 1)),
            dma((HEADS, 4, 2)),
            dma((HEADS, 3)),
            dma((HEADS, 3)),
            dma((HEADS, 2)),
            dma((HEADS,)),
            dma((HEADS, 2)),
            dma((HEADS,)),
        ],
        compiler_params=pltpu.CompilerParams(
            collective_id=0, has_side_effects=True, vmem_limit_bytes=60 * 1024 * 1024
        ),
        name="exchange_and_attend",
    )(queries, keys.reshape(split), values.reshape(split), doc_lengths, selected.T)


def solution(mesh):
    rows = P(("blk", "uly"), None)
    return jax.shard_map(
        on_device, mesh=mesh, in_specs=(rows, rows, rows, P(), P()), out_specs=rows, check_vma=False
    )
```

```python
import functools
import math

import jax
import jax.numpy as jnp
from jax import lax
from jax.experimental import pallas as pl
from jax.experimental.pallas import tpu as pltpu
from jax.sharding import PartitionSpec as P

HQ = 32
KVH = 8
HD = 128
NY = 4
GROUP = HQ // KVH
HEADS = KVH // NY
BIG = float(1 << 20)
LOG2E_SCALE = math.log2(math.e) / math.sqrt(HD)
MESH = pl.DeviceIdType.MESH


def device(x, y, z, c):
    return ((x // 2) * 8 + z * 2 + c, (x % 2) * NY + y)


def kernel(
    rows,
    q_hbm,
    k_hbm,
    v_hbm,
    lengths,
    selected,
    out_hbm,
    q_all,
    kv_own,
    gathered_00,
    gathered_01,
    gathered_10,
    gathered_11,
    relayed_00,
    relayed_01,
    relayed_10,
    relayed_11,
    picked,
    final,
    arrived_0,
    arrived_1,
    k_aug,
    v_aug,
    q_doc,
    acc_ref,
    top_ref,
    out_all,
    kv_send,
    kv_recv,
    q_send,
    q_recv,
    pre_send,
    pre_recv,
    a_send,
    a_recv,
    b_send,
    b_recv,
    c_recv,
    o_send,
    o_recv,
    local_kv,
    local_q,
    local_g,
    local_o,
):
    block = NY * rows
    quarter = rows // 4
    gathered = ((gathered_00, gathered_01), (gathered_10, gathered_11))
    relayed = ((relayed_00, relayed_01), (relayed_10, relayed_11))
    arrived = (arrived_0, arrived_1)
    blk, uly = lax.axis_index("blk"), lax.axis_index("uly")
    xh, z, c = blk // 8, (blk // 2) % 4, blk % 2
    xl, y = uly // NY, uly % NY
    x = xh * 2 + xl
    a = x * (1 - c) + z * c
    b = z * (1 - c) + x * c
    partner = device(x, y, z, 1 - c)

    def along_a(a_to):
        return device(a_to * (1 - c) + x * c, y, z * (1 - c) + a_to * c, c)

    def along_b(b_to, c_to):
        return device(x * (1 - c) + b_to * c, y, b_to * (1 - c) + z * c, c_to)

    def remote(src, dst, send, recv, to):
        return pltpu.make_async_remote_copy(
            src_ref=src, dst_ref=dst, send_sem=send, recv_sem=recv, device_id=to, device_id_type=MESH
        )

    barrier = pltpu.get_barrier_semaphore()
    friends = [partner] + [device(x, (y + k) % 4, z, c) for k in (1, 2, 3)]
    for k in (1, 3):
        for core in (0, 1):
            friends.append(device((x + k) % 4, y, z, core))
            friends.append(device(x, y, (z + k) % 4, core))
    for friend in friends:
        pl.semaphore_signal(barrier, inc=1, device_id=friend, device_id_type=MESH)

    def kv_copy(h, kv, k):
        to = (y + k) % 4
        columns = pl.ds(pl.multiple_of((to * HEADS + h) * HD, HD), HD)
        src = (k_hbm if kv == 0 else v_hbm).at[:, :, columns]
        dst = kv_own.at[h, :, kv, y]
        if k == 0:
            return pltpu.make_async_copy(src, dst, local_kv.at[h, kv])
        return remote(src, dst, kv_send.at[h, kv, k - 1], kv_recv.at[h, kv, k - 1], device(x, to, z, c))

    def q_copy(h, k):
        to = (y + k) % 4
        width = GROUP * HD
        columns = pl.ds(pl.multiple_of((to * HEADS + h) * width, width), width)
        src, dst = q_hbm.at[:, columns], q_all.at[h, y]
        if k == 0:
            return pltpu.make_async_copy(src, dst, local_q.at[h])
        return remote(src, dst, q_send.at[h, k - 1], q_recv.at[h, k - 1], device(x, to, z, c))

    def out_copy(h, t, k):
        width = GROUP * HD
        columns = pl.ds(pl.multiple_of((y * HEADS + h) * width, width), width)
        src, dst = out_all.at[h, t], out_hbm.at[:, columns]
        if k == 0:
            return pltpu.make_async_copy(src, dst, local_o.at[h])
        return remote(src, dst, o_send.at[h, k - 1], o_recv.at[h, k - 1], device(x, t, z, c))

    def near(p):
        return p + 1 - 2 * (p % 2)

    def far(p):
        return 3 - p

    def pairing(j, step):
        return (near, far)[(j + step) % 2]

    def source(k):
        return (y - k + 4) % 4

    def pre_copy(h, j, k):
        chunk = source(k)
        return remote(
            kv_own.at[h, 2 * (1 - c) + j, :, chunk],
            gathered[h][j].at[b * 2 + c, :, chunk],
            pre_send.at[h, j, k],
            pre_recv.at[h, j, k],
            partner,
        )

    def own_item(h, j):
        return pltpu.make_async_copy(kv_own.at[h, 2 * c + j], gathered[h][j].at[a * 2 + c], local_g.at[h, j])

    def first_copy(h, j, own, k=None):
        slot = a * 2 + (c if own else 1 - c)
        src = kv_own.at[h, 2 * c + j] if own else gathered[h][j].at[slot]
        dst = gathered[h][j].at[slot]
        if k is not None:
            src, dst = src.at[:, source(k)], dst.at[:, source(k)]
        index = 0 if own else 1
        return remote(
            src,
            dst,
            a_send.at[h, j, index],
            a_recv.at[h, j, index],
            along_a(pairing(j, 0)(a)),
        )

    def second_copy(h, j, own):
        place = a if own else pairing(j, 0)(a)
        pair = pl.ds(place * 2, 2)
        index = 2 if own else 3
        return remote(
            gathered[h][j].at[pair],
            gathered[h][j].at[pair],
            a_send.at[h, j, index],
            a_recv.at[h, j, index],
            along_a(pairing(j, 1)(a)),
        )

    def third_copy(h, j):
        return remote(
            picked.at[h, j], relayed[h][j], b_send.at[h, j, 0], b_recv.at[h, j, 0], along_b(pairing(j, 0)(b), c)
        )

    def fourth_copy(h, j, core):
        return remote(
            final.at[h, j, core],
            arrived[h].at[2 * c + j, 1],
            b_send.at[h, j, 1 + core],
            c_recv.at[h, 2 * c + j, 1],
            along_b(pairing(j, 1)(b), core),
        )

    def partner_copy(h, j):
        return remote(
            final.at[h, j, 2],
            arrived[h].at[2 * c + j, 0],
            b_send.at[h, j, 3],
            c_recv.at[h, 2 * c + j, 0],
            partner,
        )

    def arrival(h, unit, slot):
        return remote(
            final.at[h, 0, 0], arrived[h].at[unit, slot], b_send.at[h, 0, 1], c_recv.at[h, unit, slot], partner
        )

    def wanted(x_to, z_to, c_to, h):
        place = (x_to // 2) * 16 + z_to * 4 + c_to * 2 + x_to % 2
        pick = selected[y * HEADS + h, place]
        return pick, (pick // 16) * 2 + pick % 2, (pick // 4) % 4, (pick // 2) % 2

    def request(h, b_to, c_to):
        x_to, z_to = x * (1 - c) + b_to * c, b_to * (1 - c) + z * c
        _, x_s, z_s, c_s = wanted(x_to, z_to, c_to, h)
        return (x_s * (1 - c) + z_s * c) * 2 + c_s, z_s * (1 - c) + x_s * c

    def pick_third(h, j):
        to = pairing(j, 0)(b)
        for w, b_to in ((0, to), (1, pairing(j, 1)(to))):
            for core in (0, 1):
                picked[h, j, 2 * w + core] = gathered[h][j][request(h, b_to, core)[0]]

    def pick_fourth(h, j, w, core):
        b_to = pairing(j, 1)(b) if w else b
        index, b_s = request(h, b_to, core)
        return jnp.where(b_s == b, gathered[h][j][index], relayed[h][j][2 * w + core])

    lane = lax.broadcasted_iota(jnp.int32, (1, HD), 1)
    begin = jnp.zeros((1, HD), jnp.int32)
    end = jnp.full((1, HD), 1 << 30, jnp.int32)
    total = jnp.int32(0)
    for d in range(4):
        begin = jnp.where(lane == d, total, begin)
        total = total + lengths[d]
        end = jnp.where(lane == d, total, end)

    place_me = xh * 16 + z * 4 + c * 2 + xl

    def inside(first, n):
        p = first + lax.broadcasted_iota(jnp.int32, (n, HD), 0)
        return (p >= begin) & (p < end)

    def penalty(first, live, regrouped):
        i = lax.broadcasted_iota(jnp.int32, (block, HD), 0)
        if regrouped:
            i = (i // quarter % NY) * rows + (i // rows) * quarter + i % quarter
        p = first + i
        visible = (p >= begin) & (p < end)
        hidden = jnp.where(live, 0.0, -BIG)
        return jnp.where(visible, hidden, -BIG).astype(jnp.bfloat16)

    def scores(q_tile, keys):
        return lax.dot_general(
            q_tile, keys, (((1,), (1,)), ((), ())), preferred_element_type=jnp.float32
        )

    def query(h, t, j):
        return jnp.concatenate(
            [q_all[h, t, :, j * HD : (j + 1) * HD], q_doc[pl.ds(pl.multiple_of(t * rows, rows), rows)]], axis=1
        )

    def own_setup(h):
        for chunk in range(NY):
            for unit in range(4):
                there = slice(chunk * rows + unit * quarter, chunk * rows + (unit + 1) * quarter)
                k_aug[h, 0, there, :HD] = kv_own[h, unit, 0, chunk]
                v_aug[h, 0, there, :HD] = kv_own[h, unit, 1, chunk]
        k_aug[h, 0, :, HD:] = penalty(place_me * block, True, False)
        v_aug[h, 0, :, HD:] = jnp.ones((block, HD), jnp.bfloat16)

    def own_attention(h, tiles):
        row = lax.broadcasted_iota(jnp.int32, (rows, rows), 0)
        column = lax.broadcasted_iota(jnp.int32, (rows, rows), 1)
        for t in tiles:
            for j in range(GROUP):
                q_tile = query(h, t, j)
                last = scores(q_tile, k_aug[h, 0, t * rows : (t + 1) * rows])
                last = jnp.where(row >= column, last, -BIG)
                top = jnp.max(last, axis=1, keepdims=True)
                if t > 0:
                    first = scores(q_tile, k_aug[h, 0, : t * rows])
                    top = jnp.maximum(top, jnp.max(first, axis=1, keepdims=True))
                weight = jnp.exp2((last - top) * LOG2E_SCALE).astype(jnp.bfloat16)
                acc = jnp.dot(
                    weight, v_aug[h, 0, t * rows : (t + 1) * rows], preferred_element_type=jnp.float32
                )
                if t > 0:
                    weight = jnp.exp2((first - top) * LOG2E_SCALE).astype(jnp.bfloat16)
                    acc = acc + jnp.dot(weight, v_aug[h, 0, : t * rows], preferred_element_type=jnp.float32)
                acc_ref[h, t, j] = acc
                top_ref[h, t, j] = jnp.broadcast_to(top, (rows, HD))

    def sel_setup(h):
        pick, x_s, z_s, _ = wanted(x, z, c, h)
        live = pick != place_me
        for r, source, here in ((0, z_s, z), (1, x_s, x)):
            for j in (0, 1):
                unit = 2 * r + j
                slot = jnp.where((source == here) | (source == pairing(j, 0)(here)), 0, 1)
                both = arrived[h][unit, slot]
                there = slice(unit * rows, (unit + 1) * rows)
                k_aug[h, 1, there, :HD] = both[0].reshape(rows, HD)
                v_aug[h, 1, there, :HD] = both[1].reshape(rows, HD)
        k_aug[h, 1, :, HD:] = penalty(pick * block, live, True)
        v_aug[h, 1, :, HD:] = jnp.ones((block, HD), jnp.bfloat16)

    def sel_attention(h, t):
        for j in range(GROUP):
            s = scores(query(h, t, j), k_aug[h, 1])
            before = top_ref[h, t, j][:, :1]
            top = jnp.maximum(before, jnp.max(s, axis=1, keepdims=True))
            weight = jnp.exp2((s - top) * LOG2E_SCALE).astype(jnp.bfloat16)
            acc = jnp.dot(weight, v_aug[h, 1], preferred_element_type=jnp.float32)
            acc = acc + acc_ref[h, t, j] * jnp.exp2((before - top) * LOG2E_SCALE)
            out_all[h, t, :, j * HD : (j + 1) * HD] = (acc[:, :HD] / acc[:, HD:]).astype(jnp.bfloat16)

    for h in range(HEADS):
        for kv in (0, 1):
            kv_copy(h, kv, 0).start()
    for h in range(HEADS):
        q_copy(h, 0).start()
    q_doc[...] = jnp.where(inside(place_me * block, block), 1.0, 0.0).astype(jnp.bfloat16)
    pl.semaphore_wait(barrier, len(friends))

    def send_keys(h):
        for k in (1, 3, 2):
            for kv in (0, 1):
                if h > 0:
                    kv_copy(h - 1, kv, k).wait_send()
                kv_copy(h, kv, k).start()

    def send_queries(h):
        for k in (1, 3, 2):
            if h == 0:
                for kv in (0, 1):
                    kv_copy(HEADS - 1, kv, k).wait_send()
            else:
                q_copy(h - 1, k).wait_send()
            q_copy(h, k).start()

    def send_first(h, k):
        for kv in (0, 1):
            if k == 0:
                kv_copy(h, kv, k).wait()
            else:
                kv_copy(h, kv, k).wait_recv()
        for j in (0, 1):
            pre_copy(h, j, k).start()
        for j in (0, 1):
            first_copy(h, j, True, k).start()

    def pass_first(h, k):
        for j in (0, 1):
            pre_copy(h, j, k).wait_recv()
            first_copy(h, j, False, k).start()

    def send_second_own(h):
        for j in (0, 1):
            own_item(h, j).start()
        for j in (0, 1):
            own_item(h, j).wait()
            second_copy(h, j, True).start()

    def send_second(h):
        for j in (0, 1):
            first_copy(h, j, True).wait_recv()
            first_copy(h, j, False).wait_recv()
            second_copy(h, j, False).start()

    def send_third(h):
        for j in (0, 1):
            second_copy(h, j, True).wait_recv()
            second_copy(h, j, False).wait_recv()
            pick_third(h, j)
            third_copy(h, j).start()

    def send_fourth(h):
        for j in (0, 1):
            third_copy(h, j).wait_recv()
            for core in (0, 1):
                final[h, j, core] = pick_fourth(h, j, 1, core)
                fourth_copy(h, j, core).start()
        for j in (0, 1):
            final[h, j, 2] = jnp.where(c == 0, pick_fourth(h, j, 0, 1), pick_fourth(h, j, 0, 0))
            partner_copy(h, j).start()
            arrived[h][2 * c + j, 0] = jnp.where(c == 0, pick_fourth(h, j, 0, 0), pick_fourth(h, j, 0, 1))

    def queries_here(h):
        q_copy(h, 0).wait()
        for k in (1, 2, 3):
            q_copy(h, k).wait_recv()

    def prepare(h):
        for unit in range(4):
            arrival(h, unit, 1).wait_recv()
        for j in (0, 1):
            arrival(h, 2 * (1 - c) + j, 0).wait_recv()
        sel_setup(h)

    def give(h, ks):
        for k in ks:
            t = (y + k) % 4
            sel_attention(h, t)
            out_copy(h, t, k).start()

    send_keys(0)
    send_first(0, 0)
    send_first(1, 0)
    pass_first(0, 0)
    pass_first(1, 0)
    send_keys(1)
    send_first(0, 1)
    pass_first(0, 1)
    send_first(0, 3)
    pass_first(0, 3)
    send_first(0, 2)
    pass_first(0, 2)
    send_second_own(0)
    send_queries(0)
    own_setup(0)
    send_second(0)
    send_first(1, 1)
    pass_first(1, 1)
    send_first(1, 3)
    pass_first(1, 3)
    send_first(1, 2)
    pass_first(1, 2)
    send_second_own(1)
    own_setup(1)
    send_third(0)
    send_queries(1)
    for j in (0, 1):
        third_copy(0, j).wait_send()
    send_second(1)
    queries_here(0)
    own_attention(0, (0, 1,))
    send_fourth(0)
    own_attention(0, (2, 3,))
    send_third(1)
    prepare(0)
    give(0, (2, 1, 3, 0,))
    queries_here(1)
    own_attention(1, (0, 1, 2,))
    send_fourth(1)
    own_attention(1, (3,))
    prepare(1)
    give(1, (2, 1, 3, 0,))

    for h in range(HEADS):
        for j in (0, 1):
            for k in range(NY):
                pre_copy(h, j, k).wait_send()
            for own in (True, False):
                first_copy(h, j, own).wait_send()
                second_copy(h, j, own).wait_send()
            if h > 0:
                third_copy(h, j).wait_send()
            for core in (0, 1):
                fourth_copy(h, j, core).wait_send()
            partner_copy(h, j).wait_send()
        out_copy(h, y, 0).wait()
        for k in (1, 2, 3):
            if h > 0:
                q_copy(h, k).wait_send()
            out_copy(h, (y + k) % 4, k).wait_send()
            out_copy(h, (y + k) % 4, k).wait_recv()


def on_device(queries, keys, values, doc_lengths, selected):
    rows = queries.shape[0]
    block = NY * rows
    item = (2, NY, rows // 4, HD)
    width = GROUP * HD
    split = (4, rows // 4, keys.shape[1])
    bf16, f32 = jnp.bfloat16, jnp.float32
    dma = pltpu.SemaphoreType.DMA
    anywhere = pl.BlockSpec(memory_space=pl.ANY)
    scalars = pl.BlockSpec(memory_space=pltpu.SMEM)
    return pl.pallas_call(
        functools.partial(kernel, rows),
        out_shape=pltpu.VMEM(queries.shape, bf16),
        in_specs=[anywhere, anywhere, anywhere, scalars, scalars],
        out_specs=anywhere,
        scratch_shapes=[
            pltpu.VMEM((HEADS, NY, rows, width), bf16),
            pltpu.VMEM((HEADS, 4) + item, bf16),
            *[pltpu.VMEM((8,) + item, bf16)] * 4,
            *[pltpu.VMEM((4,) + item, bf16)] * 4,
            pltpu.VMEM((HEADS, 2, 4) + item, bf16),
            pltpu.VMEM((HEADS, 2, 3) + item, bf16),
            *[pltpu.VMEM((4, 2) + item, bf16)] * 2,
            pltpu.VMEM((HEADS, 2, block, 2 * HD), bf16),
            pltpu.VMEM((HEADS, 2, block, 2 * HD), bf16),
            pltpu.VMEM((block, HD), bf16),
            pltpu.VMEM((HEADS, NY, GROUP, rows, 2 * HD), f32),
            pltpu.VMEM((HEADS, NY, GROUP, rows, HD), f32),
            pltpu.VMEM((HEADS, NY, rows, width), bf16),
            dma((HEADS, 2, 3)),
            dma((HEADS, 2, 3)),
            dma((HEADS, 3)),
            dma((HEADS, 3)),
            dma((HEADS, 2, NY)),
            dma((HEADS, 2, NY)),
            dma((HEADS, 2, 4)),
            dma((HEADS, 2, 4)),
            dma((HEADS, 2, 4)),
            dma((HEADS, 2, 1)),
            dma((HEADS, 4, 2)),
            dma((HEADS, 3)),
            dma((HEADS, 3)),
            dma((HEADS, 2)),
            dma((HEADS,)),
            dma((HEADS, 2)),
            dma((HEADS,)),
        ],
        compiler_params=pltpu.CompilerParams(
            collective_id=0, has_side_effects=True, vmem_limit_bytes=64938 * 1000
        ),
        name="exchange_and_attend",
    )(queries, keys.reshape(split), values.reshape(split), doc_lengths, selected.T)


def solution(mesh):
    rows = P(("blk", "uly"), None)
    return jax.shard_map(
        on_device, mesh=mesh, in_specs=(rows, rows, rows, P(), P()), out_specs=rows, check_vma=False
    )
```

```python
import functools
import math

import jax
import jax.numpy as jnp
from jax import lax
from jax.experimental import pallas as pl
from jax.experimental.pallas import tpu as pltpu
from jax.sharding import PartitionSpec as P

HQ = 32
KVH = 8
HD = 128
NY = 4
GROUP = HQ // KVH
HEADS = KVH // NY
BIG = float(1 << 20)
LOG2E_SCALE = math.log2(math.e) / math.sqrt(HD)
MESH = pl.DeviceIdType.MESH


def device(x, y, z, c):
    return ((x // 2) * 8 + z * 2 + c, (x % 2) * NY + y)


def kernel(
    rows,
    q_hbm,
    k_hbm,
    v_hbm,
    lengths,
    selected,
    out_hbm,
    q_all,
    kv_own,
    gathered_00,
    gathered_01,
    gathered_10,
    gathered_11,
    relayed_00,
    relayed_01,
    relayed_10,
    relayed_11,
    picked,
    final,
    arrived_0,
    arrived_1,
    k_aug,
    v_aug,
    q_doc,
    acc_ref,
    top_ref,
    out_all,
    kv_send,
    kv_recv,
    q_send,
    q_recv,
    pre_send,
    pre_recv,
    a_send,
    a_recv,
    b_send,
    b_recv,
    c_recv,
    o_send,
    o_recv,
    local_kv,
    local_q,
    local_g,
    local_o,
):
    block = NY * rows
    quarter = rows // 4
    gathered = ((gathered_00, gathered_01), (gathered_10, gathered_11))
    relayed = ((relayed_00, relayed_01), (relayed_10, relayed_11))
    arrived = (arrived_0, arrived_1)
    blk, uly = lax.axis_index("blk"), lax.axis_index("uly")
    xh, z, c = blk // 8, (blk // 2) % 4, blk % 2
    xl, y = uly // NY, uly % NY
    x = xh * 2 + xl
    a = x * (1 - c) + z * c
    b = z * (1 - c) + x * c
    partner = device(x, y, z, 1 - c)

    def along_a(a_to):
        return device(a_to * (1 - c) + x * c, y, z * (1 - c) + a_to * c, c)

    def along_b(b_to, c_to):
        return device(x * (1 - c) + b_to * c, y, b_to * (1 - c) + z * c, c_to)

    def remote(src, dst, send, recv, to):
        return pltpu.make_async_remote_copy(
            src_ref=src, dst_ref=dst, send_sem=send, recv_sem=recv, device_id=to, device_id_type=MESH
        )

    barrier = pltpu.get_barrier_semaphore()
    friends = [partner] + [device(x, (y + k) % 4, z, c) for k in (1, 2, 3)]
    for k in (1, 3):
        for core in (0, 1):
            friends.append(device((x + k) % 4, y, z, core))
            friends.append(device(x, y, (z + k) % 4, core))
    for friend in friends:
        pl.semaphore_signal(barrier, inc=1, device_id=friend, device_id_type=MESH)

    def kv_copy(h, kv, k):
        to = (y + k) % 4
        columns = pl.ds(pl.multiple_of((to * HEADS + h) * HD, HD), HD)
        src = (k_hbm if kv == 0 else v_hbm).at[:, :, columns]
        dst = kv_own.at[h, :, kv, y]
        if k == 0:
            return pltpu.make_async_copy(src, dst, local_kv.at[h, kv])
        return remote(src, dst, kv_send.at[h, kv, k - 1], kv_recv.at[h, kv, k - 1], device(x, to, z, c))

    def q_copy(h, k):
        to = (y + k) % 4
        width = GROUP * HD
        columns = pl.ds(pl.multiple_of((to * HEADS + h) * width, width), width)
        src, dst = q_hbm.at[:, columns], q_all.at[h, y]
        if k == 0:
            return pltpu.make_async_copy(src, dst, local_q.at[h])
        return remote(src, dst, q_send.at[h, k - 1], q_recv.at[h, k - 1], device(x, to, z, c))

    def out_copy(h, t, k):
        width = GROUP * HD
        columns = pl.ds(pl.multiple_of((y * HEADS + h) * width, width), width)
        src, dst = out_all.at[h, t], out_hbm.at[:, columns]
        if k == 0:
            return pltpu.make_async_copy(src, dst, local_o.at[h])
        return remote(src, dst, o_send.at[h, k - 1], o_recv.at[h, k - 1], device(x, t, z, c))

    def near(p):
        return p + 1 - 2 * (p % 2)

    def far(p):
        return 3 - p

    def pairing(j, step):
        return (near, far)[(j + step) % 2]

    def source(k):
        return (y - k + 4) % 4

    def pre_copy(h, j, k):
        chunk = source(k)
        return remote(
            kv_own.at[h, 2 * (1 - c) + j, :, chunk],
            gathered[h][j].at[b * 2 + c, :, chunk],
            pre_send.at[h, j, k],
            pre_recv.at[h, j, k],
            partner,
        )

    def own_item(h, j):
        return pltpu.make_async_copy(kv_own.at[h, 2 * c + j], gathered[h][j].at[a * 2 + c], local_g.at[h, j])

    def first_copy(h, j, own, k=None):
        slot = a * 2 + (c if own else 1 - c)
        src = kv_own.at[h, 2 * c + j] if own else gathered[h][j].at[slot]
        dst = gathered[h][j].at[slot]
        if k is not None:
            src, dst = src.at[:, source(k)], dst.at[:, source(k)]
        index = 0 if own else 1
        return remote(
            src,
            dst,
            a_send.at[h, j, index],
            a_recv.at[h, j, index],
            along_a(pairing(j, 0)(a)),
        )

    def second_copy(h, j, own):
        place = a if own else pairing(j, 0)(a)
        pair = pl.ds(place * 2, 2)
        index = 2 if own else 3
        return remote(
            gathered[h][j].at[pair],
            gathered[h][j].at[pair],
            a_send.at[h, j, index],
            a_recv.at[h, j, index],
            along_a(pairing(j, 1)(a)),
        )

    def third_copy(h, j):
        return remote(
            picked.at[h, j], relayed[h][j], b_send.at[h, j, 0], b_recv.at[h, j, 0], along_b(pairing(j, 0)(b), c)
        )

    def fourth_copy(h, j, core):
        return remote(
            final.at[h, j, core],
            arrived[h].at[2 * c + j, 1],
            b_send.at[h, j, 1 + core],
            c_recv.at[h, 2 * c + j, 1],
            along_b(pairing(j, 1)(b), core),
        )

    def partner_copy(h, j):
        return remote(
            final.at[h, j, 2],
            arrived[h].at[2 * c + j, 0],
            b_send.at[h, j, 3],
            c_recv.at[h, 2 * c + j, 0],
            partner,
        )

    def arrival(h, unit, slot):
        return remote(
            final.at[h, 0, 0], arrived[h].at[unit, slot], b_send.at[h, 0, 1], c_recv.at[h, unit, slot], partner
        )

    def wanted(x_to, z_to, c_to, h):
        place = (x_to // 2) * 16 + z_to * 4 + c_to * 2 + x_to % 2
        pick = selected[y * HEADS + h, place]
        return pick, (pick // 16) * 2 + pick % 2, (pick // 4) % 4, (pick // 2) % 2

    def request(h, b_to, c_to):
        x_to, z_to = x * (1 - c) + b_to * c, b_to * (1 - c) + z * c
        _, x_s, z_s, c_s = wanted(x_to, z_to, c_to, h)
        return (x_s * (1 - c) + z_s * c) * 2 + c_s, z_s * (1 - c) + x_s * c

    def pick_third(h, j):
        to = pairing(j, 0)(b)
        for w, b_to in ((0, to), (1, pairing(j, 1)(to))):
            for core in (0, 1):
                picked[h, j, 2 * w + core] = gathered[h][j][request(h, b_to, core)[0]]

    def pick_fourth(h, j, w, core):
        b_to = pairing(j, 1)(b) if w else b
        index, b_s = request(h, b_to, core)
        return jnp.where(b_s == b, gathered[h][j][index], relayed[h][j][2 * w + core])

    lane = lax.broadcasted_iota(jnp.int32, (1, HD), 1)
    begin = jnp.zeros((1, HD), jnp.int32)
    end = jnp.full((1, HD), 1 << 30, jnp.int32)
    total = jnp.int32(0)
    for d in range(4):
        begin = jnp.where(lane == d, total, begin)
        total = total + lengths[d]
        end = jnp.where(lane == d, total, end)

    place_me = xh * 16 + z * 4 + c * 2 + xl

    def inside(first, n):
        p = first + lax.broadcasted_iota(jnp.int32, (n, HD), 0)
        return (p >= begin) & (p < end)

    def penalty(first, live, regrouped):
        i = lax.broadcasted_iota(jnp.int32, (block, HD), 0)
        if regrouped:
            i = (i // quarter % NY) * rows + (i // rows) * quarter + i % quarter
        p = first + i
        visible = (p >= begin) & (p < end)
        hidden = jnp.where(live, 0.0, -BIG)
        return jnp.where(visible, hidden, -BIG).astype(jnp.bfloat16)

    def scores(q_tile, keys):
        return lax.dot_general(
            q_tile, keys, (((1,), (1,)), ((), ())), preferred_element_type=jnp.float32
        )

    def query(h, t, j):
        return jnp.concatenate(
            [q_all[h, t, :, j * HD : (j + 1) * HD], q_doc[pl.ds(pl.multiple_of(t * rows, rows), rows)]], axis=1
        )

    def own_setup(h):
        for chunk in range(NY):
            for unit in range(4):
                there = slice(chunk * rows + unit * quarter, chunk * rows + (unit + 1) * quarter)
                k_aug[h, 0, there, :HD] = kv_own[h, unit, 0, chunk]
                v_aug[h, 0, there, :HD] = kv_own[h, unit, 1, chunk]
        k_aug[h, 0, :, HD:] = penalty(place_me * block, True, False)
        v_aug[h, 0, :, HD:] = jnp.ones((block, HD), jnp.bfloat16)
        pick = wanted(x, z, c, h)[0]
        k_aug[h, 1, :, HD:] = penalty(pick * block, pick != place_me, True)
        v_aug[h, 1, :, HD:] = jnp.ones((block, HD), jnp.bfloat16)

    def own_attention(h, tiles):
        row = lax.broadcasted_iota(jnp.int32, (rows, rows), 0)
        column = lax.broadcasted_iota(jnp.int32, (rows, rows), 1)
        for t in tiles:
            for j in range(GROUP):
                q_tile = query(h, t, j)
                last = scores(q_tile, k_aug[h, 0, t * rows : (t + 1) * rows])
                last = jnp.where(row >= column, last, -BIG)
                top = jnp.max(last, axis=1, keepdims=True)
                if t > 0:
                    first = scores(q_tile, k_aug[h, 0, : t * rows])
                    top = jnp.maximum(top, jnp.max(first, axis=1, keepdims=True))
                weight = jnp.exp2((last - top) * LOG2E_SCALE).astype(jnp.bfloat16)
                acc = jnp.dot(
                    weight, v_aug[h, 0, t * rows : (t + 1) * rows], preferred_element_type=jnp.float32
                )
                if t > 0:
                    weight = jnp.exp2((first - top) * LOG2E_SCALE).astype(jnp.bfloat16)
                    acc = acc + jnp.dot(weight, v_aug[h, 0, : t * rows], preferred_element_type=jnp.float32)
                acc_ref[h, t, j] = acc
                top_ref[h, t, j] = jnp.broadcast_to(top, (rows, HD))

    def sel_setup(h):
        _, x_s, z_s, _ = wanted(x, z, c, h)
        for r, source, here in ((0, z_s, z), (1, x_s, x)):
            for j in (0, 1):
                unit = 2 * r + j
                slot = jnp.where((source == here) | (source == pairing(j, 0)(here)), 0, 1)
                both = arrived[h][unit, slot]
                there = slice(unit * rows, (unit + 1) * rows)
                k_aug[h, 1, there, :HD] = both[0].reshape(rows, HD)
                v_aug[h, 1, there, :HD] = both[1].reshape(rows, HD)

    def sel_attention(h, t):
        for j in range(GROUP):
            s = scores(query(h, t, j), k_aug[h, 1])
            before = top_ref[h, t, j][:, :1]
            top = jnp.maximum(before, jnp.max(s, axis=1, keepdims=True))
            weight = jnp.exp2((s - top) * LOG2E_SCALE).astype(jnp.bfloat16)
            acc = jnp.dot(weight, v_aug[h, 1], preferred_element_type=jnp.float32)
            acc = acc + acc_ref[h, t, j] * jnp.exp2((before - top) * LOG2E_SCALE)
            out_all[h, t, :, j * HD : (j + 1) * HD] = (acc[:, :HD] / acc[:, HD:]).astype(jnp.bfloat16)

    for h in range(HEADS):
        for kv in (0, 1):
            kv_copy(h, kv, 0).start()
    for h in range(HEADS):
        q_copy(h, 0).start()
    q_doc[...] = jnp.where(inside(place_me * block, block), 1.0, 0.0).astype(jnp.bfloat16)
    pl.semaphore_wait(barrier, len(friends))

    def send_keys(h):
        for k in (1, 3, 2):
            for kv in (0, 1):
                if h > 0:
                    kv_copy(h - 1, kv, k).wait_send()
                kv_copy(h, kv, k).start()

    def send_queries(h):
        for k in (1, 3, 2):
            if h == 0:
                for kv in (0, 1):
                    kv_copy(HEADS - 1, kv, k).wait_send()
            else:
                q_copy(h - 1, k).wait_send()
            q_copy(h, k).start()

    def send_first(h, k):
        for kv in (0, 1):
            if k == 0:
                kv_copy(h, kv, k).wait()
            else:
                kv_copy(h, kv, k).wait_recv()
        for j in (0, 1):
            pre_copy(h, j, k).start()
        for j in (0, 1):
            first_copy(h, j, True, k).start()

    def pass_first(h, k):
        for j in (0, 1):
            pre_copy(h, j, k).wait_recv()
            first_copy(h, j, False, k).start()

    def send_second_own(h):
        for j in (0, 1):
            own_item(h, j).start()
        for j in (0, 1):
            own_item(h, j).wait()
            second_copy(h, j, True).start()

    def send_second(h):
        for j in (0, 1):
            first_copy(h, j, True).wait_recv()
            first_copy(h, j, False).wait_recv()
            second_copy(h, j, False).start()

    def send_third(h):
        for j in (0, 1):
            second_copy(h, j, True).wait_recv()
            second_copy(h, j, False).wait_recv()
            pick_third(h, j)
            third_copy(h, j).start()

    def send_fourth(h):
        for j in (0, 1):
            third_copy(h, j).wait_recv()
            for core in (0, 1):
                final[h, j, core] = pick_fourth(h, j, 1, core)
                fourth_copy(h, j, core).start()
        for j in (0, 1):
            final[h, j, 2] = jnp.where(c == 0, pick_fourth(h, j, 0, 1), pick_fourth(h, j, 0, 0))
            partner_copy(h, j).start()
            arrived[h][2 * c + j, 0] = jnp.where(c == 0, pick_fourth(h, j, 0, 0), pick_fourth(h, j, 0, 1))

    def queries_here(h):
        q_copy(h, 0).wait()
        for k in (1, 2, 3):
            q_copy(h, k).wait_recv()

    def prepare(h):
        for unit in range(4):
            arrival(h, unit, 1).wait_recv()
        for j in (0, 1):
            arrival(h, 2 * (1 - c) + j, 0).wait_recv()
        sel_setup(h)

    def give(h, ks):
        for k in ks:
            t = (y + k) % 4
            sel_attention(h, t)
            out_copy(h, t, k).start()

    send_keys(0)
    send_first(0, 0)
    send_first(1, 0)
    pass_first(0, 0)
    pass_first(1, 0)
    send_keys(1)
    send_first(0, 1)
    pass_first(0, 1)
    send_first(0, 3)
    pass_first(0, 3)
    send_first(0, 2)
    pass_first(0, 2)
    send_second_own(0)
    send_queries(0)
    own_setup(0)
    send_second(0)
    send_first(1, 1)
    pass_first(1, 1)
    send_first(1, 3)
    pass_first(1, 3)
    send_first(1, 2)
    pass_first(1, 2)
    send_second_own(1)
    own_setup(1)
    send_third(0)
    send_queries(1)
    for j in (0, 1):
        third_copy(0, j).wait_send()
    send_second(1)
    queries_here(0)
    own_attention(0, (0, 1,))
    send_fourth(0)
    own_attention(0, (2, 3,))
    send_third(1)
    prepare(0)
    give(0, (2, 1, 3, 0,))
    queries_here(1)
    own_attention(1, (0, 1, 2,))
    send_fourth(1)
    own_attention(1, (3,))
    prepare(1)
    give(1, (2, 1, 3, 0,))

    for h in range(HEADS):
        for j in (0, 1):
            for k in range(NY):
                pre_copy(h, j, k).wait_send()
            for own in (True, False):
                first_copy(h, j, own).wait_send()
                second_copy(h, j, own).wait_send()
            if h > 0:
                third_copy(h, j).wait_send()
            for core in (0, 1):
                fourth_copy(h, j, core).wait_send()
            partner_copy(h, j).wait_send()
        out_copy(h, y, 0).wait()
        for k in (1, 2, 3):
            if h > 0:
                q_copy(h, k).wait_send()
            out_copy(h, (y + k) % 4, k).wait_send()
            out_copy(h, (y + k) % 4, k).wait_recv()


def on_device(queries, keys, values, doc_lengths, selected):
    rows = queries.shape[0]
    block = NY * rows
    item = (2, NY, rows // 4, HD)
    width = GROUP * HD
    split = (4, rows // 4, keys.shape[1])
    bf16, f32 = jnp.bfloat16, jnp.float32
    dma = pltpu.SemaphoreType.DMA
    anywhere = pl.BlockSpec(memory_space=pl.ANY)
    scalars = pl.BlockSpec(memory_space=pltpu.SMEM)
    return pl.pallas_call(
        functools.partial(kernel, rows),
        out_shape=pltpu.VMEM(queries.shape, bf16),
        in_specs=[anywhere, anywhere, anywhere, scalars, scalars],
        out_specs=anywhere,
        scratch_shapes=[
            pltpu.VMEM((HEADS, NY, rows, width), bf16),
            pltpu.VMEM((HEADS, 4) + item, bf16),
            *[pltpu.VMEM((8,) + item, bf16)] * 4,
            *[pltpu.VMEM((4,) + item, bf16)] * 4,
            pltpu.VMEM((HEADS, 2, 4) + item, bf16),
            pltpu.VMEM((HEADS, 2, 3) + item, bf16),
            *[pltpu.VMEM((4, 2) + item, bf16)] * 2,
            pltpu.VMEM((HEADS, 2, block, 2 * HD), bf16),
            pltpu.VMEM((HEADS, 2, block, 2 * HD), bf16),
            pltpu.VMEM((block, HD), bf16),
            pltpu.VMEM((HEADS, NY, GROUP, rows, 2 * HD), f32),
            pltpu.VMEM((HEADS, NY, GROUP, rows, HD), f32),
            pltpu.VMEM((HEADS, NY, rows, width), bf16),
            dma((HEADS, 2, 3)),
            dma((HEADS, 2, 3)),
            dma((HEADS, 3)),
            dma((HEADS, 3)),
            dma((HEADS, 2, NY)),
            dma((HEADS, 2, NY)),
            dma((HEADS, 2, 4)),
            dma((HEADS, 2, 4)),
            dma((HEADS, 2, 4)),
            dma((HEADS, 2, 1)),
            dma((HEADS, 4, 2)),
            dma((HEADS, 3)),
            dma((HEADS, 3)),
            dma((HEADS, 2)),
            dma((HEADS,)),
            dma((HEADS, 2)),
            dma((HEADS,)),
        ],
        compiler_params=pltpu.CompilerParams(
            collective_id=0, has_side_effects=True, vmem_limit_bytes=64938 * 1000
        ),
        name="exchange_and_attend",
    )(queries, keys.reshape(split), values.reshape(split), doc_lengths, selected.T)


def solution(mesh):
    rows = P(("blk", "uly"), None)
    return jax.shard_map(
        on_device, mesh=mesh, in_specs=(rows, rows, rows, P(), P()), out_specs=rows, check_vma=False
    )
```
